32 devices in a mesh: row: 8 (over y, x, core), col: 4 (over z).
Axes of the slice: x: 2, y: 2, z: 4, core: 2. Of those that a mesh axis runs over, the one named last changes fastest.
Arguments:
- diag_factor: float32 [1024, 1024], P('row', 'col'), may hold values from -1 to 2.5, as said below
- panel_factor: float32 [4096, 1024], P('row', 'col'), may hold values from -0.09375 to 0.09375
- left_factor: float32 [4096, 2048], P('row', 'col'), may hold values from -0.09375 to 0.09375
- pivot_factor: float32 [1024, 2048], P('row', 'col'), may hold values from -0.1875 to 0.1875
- panel_adjoint: float32 [4096, 1024], P('row', 'col'), may hold values from -6 to 6
- left_adjoint: float32 [4096, 2048], P('row', 'col'), may hold values from -6 to 6
- pivot_adjoint: float32 [1024, 2048], P('row', 'col'), may hold values from -6 to 6
- diag_adjoint: float32 [1024, 1024], P('row', 'col'), may hold values from -6 to 6
Outputs:
- solved_panel: float32 [4096, 1024], P('row', 'col')
- left_out: float32 [4096, 2048], P('row', 'col')
- pivot_out: float32 [1024, 2048], P('row', 'col')
- diag_out: float32 [1024, 1024], P('row', 'col')
The draws below stay inside these ranges and needn't reach their ends.
Inputs may be any that keep to these rules, and one draw needn't show every extreme that they name: diag_factor is lower triangular: zero above the diagonal, diagonal entries at least 1.
All inputs are finite; a program needn't handle non-finite values.
Results may differ from the reference program's by a relative error of at most 0.000073.
Values sent between devices are 32-bit elements; how exact they have to be, the bound alone decides.
No kernel may reach another device: no remote copies, remote signals or barrier semaphores. Data moves between devices by JAX's collectives and lax.ppermute only.
A program may use at most 64 MiB of HBM per device.

```python
import jax
import jax.numpy as jnp
from jax import lax

NB = 1024
M = 4096
K = 2048


def draw_diag_factor(key, part):
    first_key, second_key = jax.random.split(jax.random.fold_in(key, 11))
    below = jnp.clip(jax.random.normal(first_key, (NB, NB), jnp.float32), -3.0, 3.0) * 0.5 / jnp.sqrt(NB * 1.0)
    middle = jax.random.uniform(second_key, (NB,), jnp.float32, 1.0, 2.0)
    row_index = lax.broadcasted_iota(jnp.int32, (NB, NB), 0)
    col_index = lax.broadcasted_iota(jnp.int32, (NB, NB), 1)
    lower = jnp.where(row_index > col_index, below, 0.0)
    return lower + jnp.where(row_index == col_index, middle[:, None], 0.0)


def block_levels(key, shape, shards, least, largest):
    factor_of = 1.0
    for position, parts in shards:
        heights = jax.random.uniform(jax.random.fold_in(jax.random.fold_in(key, 6), position), (parts,), jnp.float32, least / len(shards), largest / len(shards))
        factor_of = factor_of * jnp.repeat(jnp.exp(heights), shape[position] // parts).reshape((-1,) + (1,) * (len(shape) - 1 - position))
    return factor_of


def normal_values(stream_key, dims, spread, bound, cuts=(), held_as=jnp.bfloat16):
    values = spread * jax.random.normal(stream_key, dims, jnp.float32)
    if cuts:
        values = values * block_levels(stream_key, dims, cuts, -0.22, 0.18)
    return jnp.clip(values, -bound, bound).astype(held_as)


def setup_inputs(seed: int = 0) -> dict:
    key_list = jax.random.split(jax.random.key(seed), 9)
    diag_factor = draw_diag_factor(jax.random.fold_in(key_list[8], 71), 0)
    panel_factor = normal_values(key_list[1], (M, NB), M ** -0.5, 0.09375, ((0, 8), (1, 4)), jnp.float32)
    left_factor = normal_values(key_list[2], (M, K), M ** -0.5, 0.09375, ((0, 8), (1, 4)), jnp.float32)
    pivot_factor = normal_values(key_list[3], (NB, K), NB ** -0.5, 0.1875, ((0, 8), (1, 4)), jnp.float32)
    panel_adjoint = normal_values(key_list[4], (M, NB), 1.0, 6.0, ((0, 8), (1, 4)), jnp.float32)
    left_adjoint = normal_values(key_list[5], (M, K), 1.0, 6.0, ((0, 8), (1, 4)), jnp.float32)
    pivot_adjoint = normal_values(key_list[6], (NB, K), 1.0, 6.0, ((0, 8), (1, 4)), jnp.float32)
    diag_adjoint = normal_values(key_list[7], (NB, NB), 1.0, 6.0, ((0, 8), (1, 4)), jnp.float32)
    return dict(diag_factor=diag_factor, panel_factor=panel_factor, left_factor=left_factor, pivot_factor=pivot_factor, panel_adjoint=panel_adjoint, left_adjoint=left_adjoint, pivot_adjoint=pivot_adjoint, diag_adjoint=diag_adjoint)


def reference(diag_factor, panel_factor, left_factor, pivot_factor, panel_adjoint, left_adjoint, pivot_adjoint, diag_adjoint):
    highest = lax.Precision.HIGHEST
    solved_panel = jax.scipy.linalg.solve_triangular(diag_factor, panel_adjoint.T, trans='T', lower=True).T
    left_out = left_adjoint - jnp.dot(solved_panel.astype(jnp.float32), pivot_factor.astype(jnp.float32), precision=highest, preferred_element_type=jnp.float32)
    pivot_out = pivot_adjoint - jnp.dot(solved_panel.T.astype(jnp.float32), left_factor.astype(jnp.float32), precision=highest, preferred_element_type=jnp.float32)
    square = jnp.dot(solved_panel.T.astype(jnp.float32), panel_factor.astype(jnp.float32), precision=highest, preferred_element_type=jnp.float32)
    diag_out = diag_adjoint - jnp.tril(square)
    return (solved_panel, left_out, pivot_out, diag_out)
```

```python
import functools

import jax
import jax.numpy as jnp
from jax import lax
from jax.experimental import pallas as pl
from jax.experimental.pallas import tpu as pltpu
from jax.sharding import PartitionSpec as P


F32 = jnp.float32
BF16 = jnp.bfloat16
VMEM = pl.BlockSpec(memory_space=pltpu.VMEM)


def split(value):
    high = value.astype(BF16)
    return high, (value - high.astype(F32)).astype(BF16)


def dot3(left, right):
    multiply = functools.partial(jnp.dot, preferred_element_type=F32)
    return multiply(left[0], right[0]) + (multiply(left[0], right[1]) + multiply(left[1], right[0]))


def invert_lower(lower):
    size = lower.shape[0]
    row = lax.broadcasted_iota(jnp.int32, lower.shape, 0)
    col = lax.broadcasted_iota(jnp.int32, lower.shape, 1)
    inverse = jnp.where(row == col, 1.0 / jnp.where(row == col, lower, 1.0), 0.0)
    level = 0
    while (1 << level) < size:
        row_block, col_block = row >> level, col >> level
        off = jnp.where(((row_block & 1) == 1) & (col_block == row_block - 1), lower, 0.0)
        if level == 0:
            down = jnp.sum(inverse, axis=1, keepdims=True)
            across = jnp.sum(inverse, axis=0, keepdims=True)
            inverse = inverse - down * off * across
        else:
            parts = split(inverse)
            inverse = inverse - dot3(parts, split(dot3(split(off), parts)))
        level += 1
    return inverse


def invert_kernel(diag_ref, out_ref):
    rows, width = diag_ref.shape
    start = lax.axis_index("row") * rows
    offset = start - lax.axis_index("col") * width
    row = lax.broadcasted_iota(jnp.int32, (rows, rows), 0)
    col = lax.broadcasted_iota(jnp.int32, (rows, rows), 1)
    lower = jnp.where(row == col, 1.0, 0.0)
    for part in range(width // rows):
        lower = jnp.where(offset == part * rows, diag_ref[:, part * rows : (part + 1) * rows], lower)
    inverse = invert_lower(lower)
    for part in range(width // rows):
        cols = slice(part * rows, (part + 1) * rows)
        out_ref[:, cols] = jnp.where(offset == part * rows, inverse, diag_ref[:, cols])


def prepare_kernel(places, n_pieces, *refs):
    pieces = refs[:n_pieces]
    panel_ref, left_ref, high_ref, low_ref, side_high, side_low = refs[n_pieces:]
    here = (lax.axis_index("row"), lax.axis_index("col"))
    for piece, index, place in places:
        band, part, block = place(*here)
        high, low = split(pieces[piece][index])
        high_ref[band, block, part] = high
        low_ref[band, block, part] = low
    width = panel_ref.shape[1]
    side_high[:, :width], side_low[:, :width] = split(panel_ref[...])
    side_high[:, width:], side_low[:, width:] = split(left_ref[...])


def solve_kernel(places, n_pieces, orders, *refs):
    pieces = refs[:n_pieces]
    high_ref, low_ref, side_high, side_low = refs[n_pieces : n_pieces + 4]
    out_refs = refs[n_pieces + 4 : n_pieces + 7]
    sums = refs[n_pieces + 7 : n_pieces + 7 + len(orders)]
    work, turned_high, turned_low = refs[n_pieces + 7 + len(orders) :]
    panel_ref, solved_high, solved_low = out_refs
    here = (lax.axis_index("row"), lax.axis_index("col"))
    blocks, depth, width = work.shape
    parts, rows = high_ref.shape[2], high_ref.shape[3]
    for piece, index, place, valid in places:
        target = place(*here)
        source = pieces[piece] if index is None else pieces[piece].at[index]
        if valid is None:
            work[target] = source[...]
        else:

            @pl.when(valid(*here))
            def _(target=target, source=source):
                work[target] = source[...]

    for block in reversed(range(blocks)):
        pending = work[block]
        found = [None] * parts
        for part in reversed(range(parts)):
            tail = pending[:, part * rows : (part + 1) * rows]
            band = [ref[block, block, part] for ref in (high_ref, low_ref)]
            answer = dot3(split(tail), [b[:, part * rows : (part + 1) * rows] for b in band])
            answer_parts = split(answer)
            found[part] = (answer, *answer_parts)
            turned_high[part, block] = answer_parts[0].T
            turned_low[part, block] = answer_parts[1].T
            if part:
                pending = pending[:, : part * rows] - dot3(answer_parts, [b[:, : part * rows] for b in band])
        whole, high, low = (jnp.concatenate([f[i] for f in found], axis=1) if parts > 1 else found[0][i] for i in range(3))
        solved_high[block] = high
        solved_low[block] = low

        @pl.when(here[1] == block)
        def _(whole=whole):
            panel_ref[...] = whole

        for other in range(block):
            factor = [ref[block, other].reshape(width, width) for ref in (high_ref, low_ref)]
            work[other] = work[other] - dot3((high, low), factor)

    side = (side_high[...], side_low[...])
    for order, sum_ref in zip(orders, sums, strict=True):
        turned = [
            jnp.concatenate([ref[place(*here)] for place in order], axis=0) for ref in (turned_high, turned_low)
        ]
        sum_ref[...] = dot3(turned, side).reshape(sum_ref.shape)


def left_kernel(places, n_pieces, *refs):
    pieces = refs[:n_pieces]
    solved_high, solved_low, adjoint_ref, out_ref, pivot_high, pivot_low = refs[n_pieces:]
    here = (lax.axis_index("row"), lax.axis_index("col"))
    for piece, window, place in places:
        block, part, rows = place(*here)
        high, low = split(pieces[piece][window[0] : window[1], :])
        pivot_high[block, part, rows[0] : rows[1]] = high
        pivot_low[block, part, rows[0] : rows[1]] = low
    blocks, width = solved_high.shape[0], solved_high.shape[2]
    total = adjoint_ref[...]
    for block in range(blocks):
        factor = [ref[block].reshape(width, ref.shape[3]) for ref in (pivot_high, pivot_low)]
        total = total - dot3((solved_high[block], solved_low[block]), factor)
    out_ref[...] = total


def call(kernel, inputs, outs, scratch=(), name=None, flops=0):
    moved = sum(v.size * v.dtype.itemsize for v in (*inputs, *outs))
    return pl.pallas_call(
        kernel,
        out_shape=tuple(outs),
        in_specs=[VMEM] * len(inputs),
        out_specs=tuple([VMEM] * len(outs)),
        scratch_shapes=list(scratch),
        name=name,
        cost_estimate=pl.CostEstimate(flops=flops, bytes_accessed=moved, transcendentals=0),
    )(*inputs)


def shape(dims, dtype=F32):
    return jax.ShapeDtypeStruct(dims, dtype)


def swap(value, axis, size, distance):
    return lax.ppermute(value, axis, [(i, i ^ distance) for i in range(size)])


def gather_chips(value, n_row, cut):
    along = [swap(value, "row", n_row, 2), swap(value, "row", n_row, 4)]
    across = [swap(cut(along[0], 0), "row", n_row, 4), swap(cut(along[1], 1), "row", n_row, 2)]
    held = [value, *along, *across]
    return held + [swap(v, "row", n_row, 1) for v in held]


PIECES = ((0, None), (1, None), (2, None), (3, 0), (3, 1))


def local(
    n_row,
    n_col,
    diag_factor,
    panel_factor,
    left_factor,
    pivot_factor,
    panel_adjoint,
    left_adjoint,
    pivot_adjoint,
    diag_adjoint,
):
    rows, width = diag_factor.shape
    depth, side = panel_adjoint.shape[0], left_factor.shape[1]
    parts = width // rows
    grouped = n_row == 8 and n_col == 4 and parts == 2
    (diag_ready,) = call(invert_kernel, [diag_factor], [shape((rows, width))], name="invert")

    if grouped:
        pairs = [(i, i ^ 1) for i in range(n_col)]
        inner = [(i, j) for i, j in ((i, ((i + 1) ^ 1) - 1) for i in range(1, n_col - 1))]
        outer_got, inner_got = panel_adjoint, panel_adjoint
        panel_pieces, panel_places = [panel_adjoint], [(0, None, lambda r, c: c, None)]
        for step in range(1, n_col):
            to_outer, to_inner = inner_got, outer_got
            outer_got = lax.ppermute(to_outer, "col", pairs)
            panel_pieces.append(outer_got)

            def outer_source(r, c, step=step):
                return jnp.where(c % 2 == 0, c + step, c - step)

            panel_places.append((len(panel_pieces) - 1, None, outer_source, lambda r, c, f=outer_source: (f(r, c) >= 0) & (f(r, c) < n_col)))
            if step < n_col - 1:
                inner_got = lax.ppermute(to_inner, "col", inner)
                panel_pieces.append(inner_got)

                def inner_source(r, c, step=step):
                    return jnp.where(c % 2 == 1, c + step, c - step)

                panel_places.append((len(panel_pieces) - 1, None, inner_source, lambda r, c, f=inner_source: (f(r, c) >= 0) & (f(r, c) < n_col)))
        bands = jnp.stack([diag_ready] + [swap(diag_ready, "col", n_col, s) for s in range(1, n_col)])
        half = n_col // 2
        diag_pieces = gather_chips(bands, n_row, lambda v, i: v[i * half : (i + 1) * half])
        diag_places = []
        for core in range(2):
            for number, (chip, which) in enumerate(PIECES):
                for index in range(n_col if which is None else half):
                    distance = index + (half if which == 1 else 0)
                    diag_places.append(
                        (
                            core * len(PIECES) + number,
                            index,
                            lambda r, c, chip=chip, core=core, distance=distance: ((r // 2) ^ chip, (r % 2) ^ core, c ^ distance),
                        )
                    )
        cut = rows // 2
        pivot_pieces = gather_chips(pivot_factor, n_row, lambda v, i: v[i * cut : (i + 1) * cut])
        pivot_places = []
        for core in range(2):
            for number, (chip, which) in enumerate(PIECES):
                window = (0, rows) if which is None else (0, cut)
                target = (0, rows) if which is None else (which * cut, (which + 1) * cut)
                pivot_places.append(
                    (
                        core * len(PIECES) + number,
                        window,
                        lambda r, c, chip=chip, core=core, target=target: ((r // 2) ^ chip, (r % 2) ^ core, target),
                    )
                )
        orders = [
            [lambda r, c, chip=chip, core=core: ((r % 2) ^ core, (r // 2) ^ chip) for chip in range(n_row // 2)]
            for core in (1, 0)
        ]
        sums = [shape((n_row // 2, rows, width + side))] * 2
    else:
        panel_pieces = [lax.all_gather(panel_adjoint, "col")]
        panel_places = [(0, i, lambda r, c, i=i: i, None) for i in range(n_col)]
        diag_pieces = [lax.all_gather(lax.all_gather(diag_ready, "row"), "col")]
        diag_places = [
            (0, (j, i), lambda r, c, i=i, j=j: (i // parts, i % parts, j)) for i in range(n_row) for j in range(n_col)
        ]
        pivot_pieces = [lax.all_gather(pivot_factor, "row", axis=0, tiled=True)]
        pivot_places = [
            (0, (i * rows, (i + 1) * rows), lambda r, c, i=i: (i // parts, i % parts, (0, rows))) for i in range(n_row)
        ]
        orders = [[lambda r, c, i=i: (i % parts, i // parts) for i in range(n_row)]]
        sums = [shape((n_row * rows, width + side))]

    factor_shape = shape((n_col, n_col, parts, rows, width), BF16)
    side_shape = shape((depth, width + side), BF16)
    high, low, side_high, side_low = call(
        functools.partial(prepare_kernel, diag_places, len(diag_pieces)),
        [*diag_pieces, panel_factor, left_factor],
        [factor_shape, factor_shape, side_shape, side_shape],
        name="prepare",
    )
    solved_shape = shape((n_col, depth, width), BF16)
    whole = n_row * rows
    solved_panel, solved_high, solved_low, *partial = call(
        functools.partial(solve_kernel, panel_places, len(panel_pieces), orders),
        [*panel_pieces, high, low, side_high, side_low],
        [shape((depth, width)), solved_shape, solved_shape, *sums],
        scratch=[pltpu.VMEM((n_col, depth, width), F32)] + [pltpu.VMEM((parts, n_col, rows, depth), BF16)] * 2,
        name="solve",
        flops=3 * depth * whole * (whole + 2 * (width + side)),
    )
    (left_out,) = call(
        functools.partial(left_kernel, pivot_places, len(pivot_pieces)),
        [*pivot_pieces, solved_high, solved_low, left_adjoint],
        [shape((depth, side))],
        scratch=[pltpu.VMEM((n_col, parts, rows, side), BF16)] * 2,
        name="left",
        flops=6 * depth * whole * side,
    )

    if grouped:
        send, keep = partial
        got = swap(send, "row", n_row, 1)
        middle = (width + side) // 2
        first = [keep[0::2, :, :middle] + got[0::2, :, :middle], keep[1::2, :, :middle] + got[1::2, :, :middle]]
        second = [keep[:2, :, middle:] + got[:2, :, middle:], keep[2:, :, middle:] + got[2:, :, middle:]]
        first_got = swap(first[1], "row", n_row, 2)
        second_got = swap(second[1], "row", n_row, 4)
        first_last = swap(first[0][1] + first_got[1], "row", n_row, 4)
        second_last = swap(second[0][1] + second_got[1], "row", n_row, 2)
        summed = jnp.concatenate(
            [first[0][0] + first_got[0] + first_last, second[0][0] + second_got[0] + second_last], axis=1
        )
    else:
        summed = lax.psum_scatter(partial[0], "row", scatter_dimension=0, tiled=True)
    pivot_out = pivot_adjoint - summed[:, width:]
    global_row = lax.axis_index("row") * rows + lax.broadcasted_iota(jnp.int32, (rows, width), 0)
    global_col = lax.axis_index("col") * width + lax.broadcasted_iota(jnp.int32, (rows, width), 1)
    diag_out = diag_adjoint - jnp.where(global_col <= global_row, summed[:, :width], 0.0)
    return (solved_panel, left_out, pivot_out, diag_out)


def solution(mesh):
    spec = P("row", "col")
    return jax.shard_map(
        functools.partial(local, mesh.shape["row"], mesh.shape["col"]),
        mesh=mesh,
        in_specs=(spec,) * 8,
        out_specs=(spec,) * 4,
        check_vma=False,
    )
```
